32 devices in a mesh: gx: 4 (over y, core), gy: 2 (over x), gz: 4 (over z).
Axes of the slice: x: 2, y: 2, z: 4, core: 2. Of those that a mesh axis runs over, the one named last changes fastest.
Arguments:
- dual_ops: bfloat16 [4, 2, 4, 768, 768], P('gx', 'gy', 'gz'), may hold values from -1 to 1, as said below
- schur_ops: bfloat16 [4, 2, 4, 768, 768], P('gx', 'gy', 'gz'), may hold values from -1 to 1, as said below
- local_rhs: float32 [4, 2, 4, 768, 128], P('gx', 'gy', 'gz'), may hold values from -6 to 6
- ordering: int32 [4, 2, 4, 768], P('gx', 'gy', 'gz'), may hold values from 0 to 127, as said below
- intact: int32 [4, 2, 4, 768], P('gx', 'gy', 'gz'), may hold values from 0 to 1, as said below
Outputs:
- multipliers: float32 [4, 2, 4, 768, 128], P('gx', 'gy', 'gz')
The draws below stay inside these ranges and needn't reach their ends.
Inputs may be any that keep to these rules, and one draw needn't show every extreme that they name: `ordering`: for every subdomain and face, the 128 entries of that face form a permutation of 0 .. 127. `intact`: an entry of face -x (or -y, -z) of a subdomain equals the entry of the same shared index on face +x (+y, +z) of its cyclic neighbour across that face. `dual_ops`: each block is symmetric positive definite. `schur_ops`: each block is symmetric positive definite.
All inputs are finite; a program needn't handle non-finite values.
Results may differ from the reference program's by a relative error of at most 0.0047.
Values may be sent and summed in bfloat16 or wider, within the bound.
A program may use at most 64 MiB of HBM per device.

```python
import jax
import jax.numpy as jnp
from jax import lax

FM = 128
M = 768
LOADS = 128
ITERS = 4
NX = 4
NY = 2
NZ = 4


def draw_symmetric(key):
    count = NX * NY * NZ
    noise = jax.random.normal(key, (count, M, M), jnp.float32)
    noise = jnp.clip(noise, -4.0, 4.0) * (0.3 / M ** 0.5)
    mixed = (noise + jnp.swapaxes(noise, 1, 2)) * 0.5 ** 0.5
    identity = jnp.eye(M, dtype=jnp.float32)
    return (0.5 * (identity[None] + mixed)).reshape(NX, NY, NZ, M, M)


def draw_dual_ops(key, part):
    return draw_symmetric(jax.random.fold_in(key, 11)).astype(jnp.bfloat16)


def draw_schur_ops(key, part):
    return draw_symmetric(jax.random.fold_in(key, 23)).astype(jnp.bfloat16)


def draw_ordering(key, part):
    rows = NX * NY * NZ * 6
    scores = jax.random.randint(jax.random.fold_in(key, 31), (rows, FM), 0, 1048576, dtype=jnp.int32)
    distinct = scores * FM + jnp.arange(FM, dtype=jnp.int32)[None, :]
    perm = jnp.argsort(distinct, axis=-1, stable=True).astype(jnp.int32)
    return perm.reshape(NX, NY, NZ, M)


def draw_intact(key, part):
    bits = jax.random.randint(jax.random.fold_in(key, 47), (NX, NY, NZ, 3, FM), 0, 4, dtype=jnp.int32)
    plus = jnp.minimum(bits, 1)
    faces = jnp.stack([jnp.roll(plus[:, :, :, 0], 1, axis=0), plus[:, :, :, 0], jnp.roll(plus[:, :, :, 1], 1, axis=1), plus[:, :, :, 1], jnp.roll(plus[:, :, :, 2], 1, axis=2), plus[:, :, :, 2]], axis=3)
    return faces.reshape(NX, NY, NZ, M).astype(jnp.int32)


def block_levels(own_key, extent, cuts, smallest, high):
    factor_of = 1.0
    for dim, parts in cuts:
        heights = jax.random.uniform(jax.random.fold_in(jax.random.fold_in(own_key, 6), dim), (parts,), jnp.float32, smallest / len(cuts), high / len(cuts))
        factor_of = factor_of * jnp.repeat(jnp.exp(heights), extent[dim] // parts).reshape((-1,) + (1,) * (len(extent) - 1 - dim))
    return factor_of


def centred(stream_key, shape, width, reach, cuts=(), kind=jnp.bfloat16):
    level = block_levels(stream_key, shape, cuts, -0.22, 0.18) if cuts else 1.0
    entries = jax.random.normal(stream_key, shape, jnp.float32) * width * level
    return jnp.minimum(jnp.maximum(entries, -reach), reach).astype(kind)


def setup_inputs(seed: int = 0) -> dict:
    keys = jax.random.split(jax.random.key(seed), 6)
    dual_ops = draw_dual_ops(jax.random.fold_in(keys[5], 71), 0)
    schur_ops = draw_schur_ops(jax.random.fold_in(keys[5], 71), 0)
    local_rhs = centred(keys[2], (NX, NY, NZ, M, LOADS), 1.0, 6.0, ((0, 4), (1, 2), (2, 4)), jnp.float32)
    ordering = draw_ordering(jax.random.fold_in(keys[5], 71), 0)
    intact = draw_intact(jax.random.fold_in(keys[5], 71), 0)
    return dict(dual_ops=dual_ops, schur_ops=schur_ops, local_rhs=local_rhs, ordering=ordering, intact=intact)


def assemble(partial_value, order, keep):
    blocks = partial_value.reshape(NX, NY, NZ, 6, FM, LOADS)
    inverse = jnp.argsort(order, axis=-1).astype(jnp.int32)
    shared = jnp.take_along_axis(blocks, inverse[..., None], axis=4)
    across = jnp.stack([
        jnp.roll(shared[:, :, :, 1], 1, axis=0),
        jnp.roll(shared[:, :, :, 0], -1, axis=0),
        jnp.roll(shared[:, :, :, 3], 1, axis=1),
        jnp.roll(shared[:, :, :, 2], -1, axis=1),
        jnp.roll(shared[:, :, :, 5], 1, axis=2),
        jnp.roll(shared[:, :, :, 4], -1, axis=2)], axis=3)
    total = (shared.astype(jnp.float32) + across.astype(jnp.float32)) * keep
    local = jnp.take_along_axis(total, order[..., None], axis=4)
    return local.reshape(NX, NY, NZ, M, LOADS)


def apply_blocks(ops, vec):
    flat_ops = ops.reshape(NX * NY * NZ, M, M)
    flat_vec = vec.reshape(NX * NY * NZ, M, LOADS)

    def one(pair):
        return jnp.dot(pair[0].astype(jnp.float32), pair[1].astype(jnp.float32), precision=lax.Precision.HIGHEST)

    out = lax.map(one, (flat_ops, flat_vec))
    return out.reshape(NX, NY, NZ, M, LOADS)


def reference(dual_ops, schur_ops, local_rhs, ordering, intact):
    order = ordering.reshape(NX, NY, NZ, 6, FM).astype(jnp.int32)
    keep = intact.reshape(NX, NY, NZ, 6, FM, 1).astype(jnp.float32)
    low, high = 0.2, 2.5
    theta = (high + low) / 2.0
    delta = (high - low) / 2.0
    sigma = theta / delta
    rho = 1.0 / sigma
    multipliers = jnp.zeros((NX, NY, NZ, M, LOADS), jnp.float32)
    update = jnp.zeros((NX, NY, NZ, M, LOADS), jnp.float32)
    for step in range(ITERS):
        if step == 0:
            partial_value = local_rhs.astype(jnp.bfloat16)
        else:
            product = apply_blocks(dual_ops, multipliers.astype(jnp.bfloat16))
            partial_value = (local_rhs - product).astype(jnp.bfloat16)
        residual = assemble(partial_value, order, keep)
        schur_part = apply_blocks(schur_ops, residual.astype(jnp.bfloat16)).astype(jnp.bfloat16)
        precond = assemble(schur_part, order, keep)
        if step == 0:
            update = precond / theta
        else:
            rho_new = 1.0 / (2.0 * sigma - rho)
            update = (rho_new * rho) * update + (2.0 * rho_new / delta) * precond
            rho = rho_new
        multipliers = multipliers + update
    return multipliers
```

```python
import functools

import jax
import jax.numpy as jnp
from jax import lax
from jax.experimental import pallas as pl
from jax.experimental.pallas import tpu as pltpu
from jax.sharding import PartitionSpec as P

ITERS = 4
AXES = ("gx", "gy", "gz")
F32 = jnp.float32
BF16 = jnp.bfloat16


def chebyshev():
    low, high = (0.2, 2.5)
    theta = (high + low) / 2.0
    delta = (high - low) / 2.0
    sigma = theta / delta
    rho = 1.0 / sigma
    factors = [(0.0, 1.0 / theta)]
    for _ in range(1, ITERS):
        rho_new = 1.0 / (2.0 * sigma - rho)
        factors.append((rho_new * rho, 2.0 * rho_new / delta))
        rho = rho_new
    return factors


def dot(a, b):
    return jnp.dot(a, b, preferred_element_type=F32)


def dot_nt(a, b):
    return lax.dot_general(a, b, (((1,), (1,)), ((), ())), preferred_element_type=F32)


def split3(x):
    hi = x.astype(BF16)
    rest = x - hi.astype(F32)
    mid = rest.astype(BF16)
    low = (rest - mid.astype(F32)).astype(BF16)
    return hi, mid, low


def kernel(
    counts, face, order_hbm, intact_hbm, rhs_hbm, schur_hbm, dual_hbm, out_hbm,
    order, intact, rhs, schur, dual, schur_sh, dual_sh, stage, rhs_sh, perm, perm_t,
    acc, vec, mult, update, base, sent, held, load_sem, out_sem, send_sem, recv_sem,
):
    wide = 2 * face
    steps = 2 * ITERS

    def neighbour(f):
        axis = AXES[f // 2]
        count = counts[f // 2]
        shift = count - 1 if f % 2 == 0 else 1
        return {axis: lax.rem(lax.axis_index(axis) + shift, count)}

    near = [neighbour(f) for f in range(6)]

    def remote(e, f):
        return pltpu.make_async_remote_copy(
            src_ref=sent.at[e, f],
            dst_ref=held.at[e, f ^ 1],
            send_sem=send_sem.at[e, f],
            recv_sem=recv_sem.at[e, f ^ 1],
            device_id=near[f],
            device_id_type=pl.DeviceIdType.MESH,
        )

    loads = [
        pltpu.make_async_copy(src, dst, load_sem.at[i])
        for i, (src, dst) in enumerate(
            [(order_hbm, order), (intact_hbm, intact), (rhs_hbm, rhs), (schur_hbm, schur), (dual_hbm, dual)]
        )
    ]
    for load in loads:
        load.start()
    barrier = pltpu.get_barrier_semaphore()
    for f in range(6):
        pl.semaphore_signal(barrier, inc=1, device_id=near[f], device_id_type=pl.DeviceIdType.MESH)

    def rows(g):
        return pl.ds(g * wide, wide)

    def pair(ref, e, g):
        return ref[e, 2 * g : 2 * g + 2].reshape(wide, ref.shape[3])

    def send(e, g, value):
        half = value.astype(BF16)
        for s in range(2):
            f = 2 * g + s
            sent[e, f] = half[s * face : (s + 1) * face]
            remote(e, f).start()

    def receive(e, g):
        for f in (2 * g, 2 * g + 1):
            remote(e, f ^ 1).wait_recv()
        return pair(sent, e, g).astype(F32) + pair(held, e, g).astype(F32)

    loads[0].wait()
    loads[1].wait()
    sub = lax.broadcasted_iota(jnp.int32, (wide, wide), 0)
    lane = lax.broadcasted_iota(jnp.int32, (1, wide), 1)
    offset = jnp.where(lane >= face, face, 0)
    for g in range(3):
        target = order[:, rows(g)] + offset
        match = sub == target
        plain = jnp.where(match, 1.0, 0.0).astype(BF16)
        keep = jnp.broadcast_to(intact[:, rows(g)], (16, wide)).astype(F32).astype(BF16)
        keep_local = dot(keep, plain)[0:1]
        perm[g] = jnp.where(match, keep_local, 0.0).astype(BF16)
    loads[2].wait()
    first = {}
    for g in (2, 1, 0):
        first[g] = dot(perm[g], rhs[rows(g), :].astype(BF16))
    pl.semaphore_wait(barrier, 6)
    for g in (2, 1, 0):
        send(0, g, first[g])

    def conjugate(src, dst, sign):
        for g in range(3):
            stage[rows(g), :] = dot(perm[g], src[rows(g), :]).astype(BF16)
        for g in range(3):
            moved = dot_nt(stage[:, rows(g)], perm[g])
            dst[:, rows(g)] = (moved if sign > 0 else -moved).astype(BF16)

    loads[3].wait()
    conjugate(schur, schur_sh, 1)

    def matvec(e, ops, offset_ref, incoming):
        for g in (0, 1, 2):
            vec[rows(g), :] = incoming(g).astype(BF16)
            if g < 2:
                value = dot(ops[:, rows(g)], vec[rows(g), :])
                if g == 0:
                    acc[...] = value if offset_ref is None else value + offset_ref[...]
                else:
                    acc[...] += value
        for g in (2, 1, 0):
            send(e, g, acc[rows(g), :] + dot(ops[rows(g), rows(2)], vec[rows(2), :]))

    factors = chebyshev()
    for step in range(ITERS):
        e = 2 * step
        if step > 0:
            old, new = factors[step - 1]

            def incoming_multipliers(g, e=e, step=step, old=old, new=new):
                value = new * receive(e - 1, g)
                if step > 1:
                    value = value + old * update[rows(g), :]
                update[rows(g), :] = value
                if step > 1:
                    value = value + mult[rows(g), :]
                mult[rows(g), :] = value
                return value

            matvec(e, dual_sh, rhs_sh, incoming_multipliers)
        matvec(e + 1, schur_sh, None, functools.partial(receive, e))
        if step == 0:
            loads[4].wait()
            conjugate(dual, dual_sh, -1)
            eye = jnp.where(sub == lax.broadcasted_iota(jnp.int32, (wide, wide), 1), 1.0, 0.0).astype(BF16)
            for g in range(3):
                hi, mid, low = split3(rhs[rows(g), :])
                rhs_sh[rows(g), :] = dot(perm[g], hi) + dot(perm[g], mid) + dot(perm[g], low)
                perm_t[g] = dot_nt(eye, perm[g]).astype(BF16)

    last = steps - 1
    old, new = factors[-1]
    for g in range(3):
        hi, mid, low = split3(mult[rows(g), :] + old * update[rows(g), :])
        kept = dot(perm_t[g], hi) + dot(perm_t[g], mid) + dot(perm_t[g], low)
        base[rows(g), :] = kept + new * dot(perm_t[g], pair(sent, last, g))
    stores = []
    for g in range(3):
        for f in (2 * g, 2 * g + 1):
            remote(last, f ^ 1).wait_recv()
        base[rows(g), :] += new * dot(perm_t[g], pair(held, last, g))
        store = pltpu.make_async_copy(base.at[rows(g), :], out_hbm.at[rows(g), :], out_sem.at[g])
        store.start()
        stores.append(store)
    for e in range(steps):
        for f in range(6):
            remote(e, f).wait_send()
    for store in stores:
        store.wait()


def local(counts, dual_ops, schur_ops, local_rhs, ordering, intact):
    size, loads = local_rhs.shape[3:]
    face = size // 6
    wide = 2 * face
    steps = 2 * ITERS
    dual = dual_ops.reshape(size, size)
    schur = schur_ops.reshape(size, size)
    rhs = local_rhs.reshape(size, loads)
    vmem = pltpu.VMEM
    out = pl.pallas_call(
        functools.partial(kernel, counts, face),
        out_shape=jax.ShapeDtypeStruct((size, loads), F32),
        in_specs=[pl.BlockSpec(memory_space=pl.ANY)] * 5,
        out_specs=pl.BlockSpec(memory_space=pl.ANY),
        scratch_shapes=[
            vmem((1, size), jnp.int32),
            vmem((1, size), jnp.int32),
            vmem((size, loads), F32),
            vmem((size, size), BF16),
            vmem((size, size), BF16),
            vmem((size, size), BF16),
            vmem((size, size), BF16),
            vmem((size, size), BF16),
            vmem((size, loads), F32),
            vmem((3, wide, wide), BF16),
            vmem((3, wide, wide), BF16),
            vmem((size, loads), F32),
            vmem((size, loads), BF16),
            vmem((size, loads), F32),
            vmem((size, loads), F32),
            vmem((size, loads), F32),
            vmem((steps, 6, face, loads), BF16),
            vmem((steps, 6, face, loads), BF16),
            pltpu.SemaphoreType.DMA((5,)),
            pltpu.SemaphoreType.DMA((3,)),
            pltpu.SemaphoreType.DMA((steps, 6)),
            pltpu.SemaphoreType.DMA((steps, 6)),
        ],
        compiler_params=pltpu.CompilerParams(
            collective_id=0, has_side_effects=True, vmem_limit_bytes=60 * 1024 * 1024
        ),
        name="feti",
    )(ordering.reshape(1, size), intact.reshape(1, size), rhs, schur, dual)
    return out.reshape(1, 1, 1, size, loads)


def solution(mesh):
    counts = tuple(mesh.shape[axis] for axis in AXES)
    in_specs = (
        P("gx", "gy", "gz", None, None),
        P("gx", "gy", "gz", None, None),
        P("gx", "gy", "gz", None, None),
        P("gx", "gy", "gz", None),
        P("gx", "gy", "gz", None),
    )
    out_specs = P("gx", "gy", "gz", None, None)
    return jax.shard_map(
        functools.partial(local, counts), mesh=mesh, in_specs=in_specs, out_specs=out_specs, check_vma=False
    )
```

```python
import functools

import jax
import jax.numpy as jnp
from jax import lax
from jax.experimental import pallas as pl
from jax.experimental.pallas import tpu as pltpu
from jax.sharding import PartitionSpec as P

ITERS = 4
AXES = ("gx", "gy", "gz")
F32 = jnp.float32
BF16 = jnp.bfloat16


def chebyshev():
    low, high = (0.2, 2.5)
    theta = (high + low) / 2.0
    delta = (high - low) / 2.0
    sigma = theta / delta
    rho = 1.0 / sigma
    factors = [(0.0, 1.0 / theta)]
    for _ in range(1, ITERS):
        rho_new = 1.0 / (2.0 * sigma - rho)
        factors.append((rho_new * rho, 2.0 * rho_new / delta))
        rho = rho_new
    return factors


def dot(a, b):
    return jnp.dot(a, b, preferred_element_type=F32)


def dot_nt(a, b):
    return lax.dot_general(a, b, (((1,), (1,)), ((), ())), preferred_element_type=F32)


def split3(x):
    hi = x.astype(BF16)
    rest = x - hi.astype(F32)
    mid = rest.astype(BF16)
    low = (rest - mid.astype(F32)).astype(BF16)
    return hi, mid, low


def kernel(
    counts, face, order_hbm, intact_hbm, rhs_hbm, schur_hbm, dual_hbm, out,
    order, intact, rhs, schur, dual, schur_sh, dual_sh, stage, rhs_sh, perm, perm_t,
    acc, mult, update, base, sent, held, load_sem, send_sem, recv_sem,
):
    wide = 2 * face
    steps = 2 * ITERS

    def neighbour(f):
        axis = AXES[f // 2]
        count = counts[f // 2]
        shift = count - 1 if f % 2 == 0 else 1
        return {axis: lax.rem(lax.axis_index(axis) + shift, count)}

    near = [neighbour(f) for f in range(6)]

    half = sent.shape[3]

    def remote(e, h, f):
        return pltpu.make_async_remote_copy(
            src_ref=sent.at[e, h, f],
            dst_ref=held.at[e, h, f ^ 1],
            send_sem=send_sem.at[e, h, f],
            recv_sem=recv_sem.at[e, h, f ^ 1],
            device_id=near[f],
            device_id_type=pl.DeviceIdType.MESH,
        )

    loads = [
        pltpu.make_async_copy(src, dst, load_sem.at[i])
        for i, (src, dst) in enumerate(
            [(order_hbm, order), (intact_hbm, intact), (rhs_hbm, rhs), (schur_hbm, schur), (dual_hbm, dual)]
        )
    ]
    for load in loads:
        load.start()
    barrier = pltpu.get_barrier_semaphore()
    for f in range(6):
        pl.semaphore_signal(barrier, inc=1, device_id=near[f], device_id_type=pl.DeviceIdType.MESH)

    def rows(g):
        return pl.ds(g * wide, wide)

    def loads_of(h):
        return pl.ds(h * half, half)

    def pair(ref, e, h, g):
        return jnp.concatenate([ref[e, h, 2 * g], ref[e, h, 2 * g + 1]], axis=1)

    def send(e, h, g, value):
        rounded = value.astype(BF16)
        for s in range(2):
            f = 2 * g + s
            sent[e, h, f] = rounded[:, s * face : (s + 1) * face]
            remote(e, h, f).start()

    def receive(e, h, g):
        for f in (2 * g, 2 * g + 1):
            remote(e, h, f ^ 1).wait_recv()
        return pair(sent, e, h, g).astype(F32) + pair(held, e, h, g).astype(F32)

    loads[0].wait()
    loads[1].wait()
    sub = lax.broadcasted_iota(jnp.int32, (wide, wide), 0)
    lane = lax.broadcasted_iota(jnp.int32, (1, wide), 1)
    offset = jnp.where(lane >= face, face, 0)
    for g in range(3):
        target = order[:, rows(g)] + offset
        match = sub == target
        plain = jnp.where(match, 1.0, 0.0).astype(BF16)
        keep = jnp.broadcast_to(intact[:, rows(g)], (16, wide)).astype(F32).astype(BF16)
        keep_local = dot(keep, plain)[0:1]
        perm[g] = jnp.where(match, keep_local, 0.0).astype(BF16)
    loads[2].wait()
    first = {}
    for g in (2, 1, 0):
        first[g] = jnp.transpose(dot(perm[g], rhs[rows(g), :].astype(BF16)))
    pl.semaphore_wait(barrier, 6)
    for h in range(2):
        for g in (2, 1, 0):
            send(0, h, g, first[g][h * half : (h + 1) * half])

    def conjugate(src, dst, sign):
        for g in range(3):
            stage[rows(g), :] = dot(perm[g], src[rows(g), :]).astype(BF16)
        for g in range(3):
            moved = dot_nt(stage[:, rows(g)], perm[g])
            dst[:, rows(g)] = (moved if sign > 0 else -moved).astype(BF16)

    loads[3].wait()
    conjugate(schur, schur_sh, 1)

    def matvec(e, h, ops, offset_ref, incoming):
        part = loads_of(h)
        for g in range(3):
            vector = incoming(h, g).astype(BF16)
            if g < 2:
                value = dot(vector, ops[rows(g), :])
                if g == 0:
                    acc[part, :] = value if offset_ref is None else value + offset_ref[part, :]
                else:
                    acc[part, :] += value
        for g in (2, 1, 0):
            send(e, h, g, acc[part, rows(g)] + dot(vector, ops[rows(2), rows(g)]))

    factors = chebyshev()
    for step in range(ITERS):
        e = 2 * step
        if step > 0:
            old, new = factors[step - 1]

            def incoming_multipliers(h, g, e=e, step=step, old=old, new=new):
                at = (loads_of(h), rows(g))
                value = new * receive(e - 1, h, g)
                if step > 1:
                    value = value + old * update[at]
                update[at] = value
                if step > 1:
                    value = value + mult[at]
                mult[at] = value
                return value

            for h in range(2):
                matvec(e, h, dual_sh, rhs_sh, incoming_multipliers)
        for h in range(2):
            matvec(e + 1, h, schur_sh, None, functools.partial(receive, e))
        if step == 0:
            loads[4].wait()
            conjugate(dual, dual_sh, -1)
            eye = jnp.where(sub == lax.broadcasted_iota(jnp.int32, (wide, wide), 1), 1.0, 0.0).astype(BF16)
            for g in range(3):
                hi, mid, low = split3(rhs[rows(g), :])
                rhs_sh[:, rows(g)] = jnp.transpose(dot(perm[g], hi) + dot(perm[g], mid) + dot(perm[g], low))
                perm_t[g] = dot_nt(eye, perm[g]).astype(BF16)

    last = steps - 1
    old, new = factors[-1]

    def both(ref, g):
        return jnp.concatenate([pair(ref, last, 0, g), pair(ref, last, 1, g)], axis=0)

    for g in range(3):
        hi, mid, low = split3(mult[:, rows(g)] + old * update[:, rows(g)])
        kept = dot_nt(perm_t[g], hi) + dot_nt(perm_t[g], mid) + dot_nt(perm_t[g], low)
        base[rows(g), :] = kept + new * dot_nt(perm_t[g], both(sent, g))
    for g in range(3):
        for h in range(2):
            for f in (2 * g, 2 * g + 1):
                remote(last, h, f ^ 1).wait_recv()
        out[rows(g), :] = base[rows(g), :] + new * dot_nt(perm_t[g], both(held, g))
    for e in range(steps):
        for h in range(2):
            for f in range(6):
                remote(e, h, f).wait_send()


def local(counts, dual_ops, schur_ops, local_rhs, ordering, intact):
    size, loads = local_rhs.shape[3:]
    face = size // 6
    wide = 2 * face
    steps = 2 * ITERS
    dual = dual_ops.reshape(size, size)
    schur = schur_ops.reshape(size, size)
    rhs = local_rhs.reshape(size, loads)
    vmem = pltpu.VMEM
    out = pl.pallas_call(
        functools.partial(kernel, counts, face),
        out_shape=jax.ShapeDtypeStruct((size, loads), F32),
        in_specs=[pl.BlockSpec(memory_space=pl.ANY)] * 5,
        out_specs=pl.BlockSpec(memory_space=pltpu.VMEM),
        scratch_shapes=[
            vmem((1, size), jnp.int32),
            vmem((1, size), jnp.int32),
            vmem((size, loads), F32),
            vmem((size, size), BF16),
            vmem((size, size), BF16),
            vmem((size, size), BF16),
            vmem((size, size), BF16),
            vmem((size, size), BF16),
            vmem((loads, size), F32),
            vmem((3, wide, wide), BF16),
            vmem((3, wide, wide), BF16),
            vmem((loads, size), F32),
            vmem((loads, size), F32),
            vmem((loads, size), F32),
            vmem((size, loads), F32),
            vmem((steps, 2, 6, loads // 2, face), BF16),
            vmem((steps, 2, 6, loads // 2, face), BF16),
            pltpu.SemaphoreType.DMA((5,)),
            pltpu.SemaphoreType.DMA((steps, 2, 6)),
            pltpu.SemaphoreType.DMA((steps, 2, 6)),
        ],
        compiler_params=pltpu.CompilerParams(
            collective_id=0, has_side_effects=True, vmem_limit_bytes=56000000
        ),
        name="feti",
    )(ordering.reshape(1, size), intact.reshape(1, size), rhs, schur, dual)
    return out.reshape(1, 1, 1, size, loads)


def solution(mesh):
    counts = tuple(mesh.shape[axis] for axis in AXES)
    in_specs = (
        P("gx", "gy", "gz", None, None),
        P("gx", "gy", "gz", None, None),
        P("gx", "gy", "gz", None, None),
        P("gx", "gy", "gz", None),
        P("gx", "gy", "gz", None),
    )
    out_specs = P("gx", "gy", "gz", None, None)
    return jax.shard_map(
        functools.partial(local, counts), mesh=mesh, in_specs=in_specs, out_specs=out_specs, check_vma=False
    )
```

```python
import functools

import jax
import jax.numpy as jnp
from jax import lax
from jax.experimental import pallas as pl
from jax.experimental.pallas import tpu as pltpu
from jax.sharding import PartitionSpec as P

ITERS = 4
AXES = ("gx", "gy", "gz")
F32 = jnp.float32
BF16 = jnp.bfloat16


def chebyshev():
    low, high = (0.2, 2.5)
    theta = (high + low) / 2.0
    delta = (high - low) / 2.0
    sigma = theta / delta
    rho = 1.0 / sigma
    factors = [(0.0, 1.0 / theta)]
    for _ in range(1, ITERS):
        rho_new = 1.0 / (2.0 * sigma - rho)
        factors.append((rho_new * rho, 2.0 * rho_new / delta))
        rho = rho_new
    return factors


def dot(a, b):
    return jnp.dot(a, b, preferred_element_type=F32)


def dot_nt(a, b):
    return lax.dot_general(a, b, (((1,), (1,)), ((), ())), preferred_element_type=F32)


def split3(x):
    hi = x.astype(BF16)
    rest = x - hi.astype(F32)
    mid = rest.astype(BF16)
    low = (rest - mid.astype(F32)).astype(BF16)
    return hi, mid, low


def kernel(
    counts, face, order_hbm, intact_hbm, rhs_hbm, schur_hbm, dual_hbm, out,
    order, intact, rhs, schur, dual, schur_sh, dual_sh, stage, rhs_sh, perm, perm_t,
    acc, mult, update, base, sent, held, load_sem, send_sem, recv_sem,
):
    wide = 2 * face
    steps = 2 * ITERS

    def neighbour(f):
        axis = AXES[f // 2]
        count = counts[f // 2]
        shift = count - 1 if f % 2 == 0 else 1
        return {axis: lax.rem(lax.axis_index(axis) + shift, count)}

    near = [neighbour(f) for f in range(6)]

    half = sent.shape[3]

    def remote(e, h, f):
        return pltpu.make_async_remote_copy(
            src_ref=sent.at[e, h, f],
            dst_ref=held.at[e, h, f ^ 1],
            send_sem=send_sem.at[e, h, f],
            recv_sem=recv_sem.at[e, h, f ^ 1],
            device_id=near[f],
            device_id_type=pl.DeviceIdType.MESH,
        )

    loads = [
        pltpu.make_async_copy(src, dst, load_sem.at[i])
        for i, (src, dst) in enumerate(
            [(order_hbm, order), (intact_hbm, intact), (rhs_hbm, rhs), (schur_hbm, schur), (dual_hbm, dual)]
        )
    ]
    for load in loads:
        load.start()
    barrier = pltpu.get_barrier_semaphore()
    for f in range(6):
        pl.semaphore_signal(barrier, inc=1, device_id=near[f], device_id_type=pl.DeviceIdType.MESH)

    def rows(g):
        return pl.ds(g * wide, wide)

    def loads_of(h):
        return pl.ds(h * half, half)

    def pair(ref, e, h, g):
        return jnp.concatenate([ref[e, h, 2 * g], ref[e, h, 2 * g + 1]], axis=1)

    def send(e, h, g, value):
        rounded = value.astype(BF16)
        for s in range(2):
            f = 2 * g + s
            sent[e, h, f] = rounded[:, s * face : (s + 1) * face]
            remote(e, h, f).start()

    def arrive(e, h, g):
        for f in (2 * g, 2 * g + 1):
            remote(e, h, f ^ 1).wait_recv()
        return pair(held, e, h, g).astype(F32)

    def residual(e, h, g):
        own = pair(sent, e, h, g).astype(F32)

        def finish():
            return (own + arrive(e, h, g)).astype(BF16), lambda: None

        return finish

    loads[0].wait()
    loads[1].wait()
    sub = lax.broadcasted_iota(jnp.int32, (wide, wide), 0)
    lane = lax.broadcasted_iota(jnp.int32, (1, wide), 1)
    offset = jnp.where(lane >= face, face, 0)
    for g in range(3):
        target = order[:, rows(g)] + offset
        match = sub == target
        plain = jnp.where(match, 1.0, 0.0).astype(BF16)
        keep = jnp.broadcast_to(intact[:, rows(g)], (16, wide)).astype(F32).astype(BF16)
        keep_local = dot(keep, plain)[0:1]
        perm[g] = jnp.where(match, keep_local, 0.0).astype(BF16)
    loads[2].wait()
    first = {}
    for g in (2, 1, 0):
        first[g] = jnp.transpose(dot(perm[g], rhs[rows(g), :].astype(BF16)))
    pl.semaphore_wait(barrier, 6)
    for h in range(2):
        for g in (2, 1, 0):
            send(0, h, g, first[g][h * half : (h + 1) * half])

    def conjugate(src, dst, sign):
        for g in range(3):
            stage[rows(g), :] = dot(perm[g], src[rows(g), :]).astype(BF16)
        for g in range(3):
            moved = dot_nt(stage[:, rows(g)], perm[g])
            dst[:, rows(g)] = (moved if sign > 0 else -moved).astype(BF16)

    loads[3].wait()
    conjugate(schur, schur_sh, 1)

    def matvec(e, h, ops, offset_ref, begin):
        part = loads_of(h)
        low = []
        for g in range(2):
            vector, later = begin(h, g)()
            low.append(vector)
            later()
        value = dot(jnp.concatenate(low, axis=1), ops[pl.ds(0, 2 * wide), :])
        acc[part, :] = value if offset_ref is None else value + offset_ref[part, :]
        finish = begin(h, 2)
        ready, weights = acc[part, rows(2)], ops[rows(2), rows(2)]
        vector, later = finish()
        send(e, h, 2, ready + dot(vector, weights))
        for g in (1, 0):
            send(e, h, g, acc[part, rows(g)] + dot(vector, ops[rows(2), rows(g)]))
        later()

    factors = chebyshev()
    for step in range(ITERS):
        e = 2 * step
        if step > 0:
            old, new = factors[step - 1]

            def multipliers(h, g, e=e, step=step, old=old, new=new):
                at = (loads_of(h), rows(g))
                change = new * pair(sent, e - 1, h, g).astype(F32)
                if step > 1:
                    change = change + old * update[at]
                total = change if step == 1 else change + mult[at]

                def finish():
                    rest = new * arrive(e - 1, h, g)
                    value = total + rest

                    def later():
                        update[at] = change + rest
                        mult[at] = value

                    return value.astype(BF16), later

                return finish

            for h in range(2):
                matvec(e, h, dual_sh, rhs_sh, multipliers)
        for h in range(2):
            matvec(e + 1, h, schur_sh, None, functools.partial(residual, e))
        if step == 0:
            loads[4].wait()
            conjugate(dual, dual_sh, -1)
            eye = jnp.where(sub == lax.broadcasted_iota(jnp.int32, (wide, wide), 1), 1.0, 0.0).astype(BF16)
            for g in range(3):
                hi, mid, low = split3(rhs[rows(g), :])
                rhs_sh[:, rows(g)] = jnp.transpose(dot(perm[g], hi) + dot(perm[g], mid) + dot(perm[g], low))
                perm_t[g] = dot_nt(eye, perm[g]).astype(BF16)

    last = steps - 1
    old, new = factors[-1]

    def both(ref, g):
        return jnp.concatenate([pair(ref, last, 0, g), pair(ref, last, 1, g)], axis=0)

    for g in range(3):
        hi, mid, low = split3(mult[:, rows(g)] + old * update[:, rows(g)])
        kept = dot_nt(perm_t[g], hi) + dot_nt(perm_t[g], mid) + dot_nt(perm_t[g], low)
        base[rows(g), :] = kept + new * dot_nt(perm_t[g], both(sent, g))
    for g in range(3):
        for h in range(2):
            for f in (2 * g, 2 * g + 1):
                remote(last, h, f ^ 1).wait_recv()
        out[rows(g), :] = base[rows(g), :] + new * dot_nt(perm_t[g], both(held, g))
    for e in range(steps):
        for h in range(2):
            for f in range(6):
                remote(e, h, f).wait_send()


def local(counts, dual_ops, schur_ops, local_rhs, ordering, intact):
    size, loads = local_rhs.shape[3:]
    face = size // 6
    wide = 2 * face
    steps = 2 * ITERS
    dual = dual_ops.reshape(size, size)
    schur = schur_ops.reshape(size, size)
    rhs = local_rhs.reshape(size, loads)
    vmem = pltpu.VMEM
    out = pl.pallas_call(
        functools.partial(kernel, counts, face),
        out_shape=jax.ShapeDtypeStruct((size, loads), F32),
        in_specs=[pl.BlockSpec(memory_space=pl.ANY)] * 5,
        out_specs=pl.BlockSpec(memory_space=pltpu.VMEM),
        scratch_shapes=[
            vmem((1, size), jnp.int32),
            vmem((1, size), jnp.int32),
            vmem((size, loads), F32),
            vmem((size, size), BF16),
            vmem((size, size), BF16),
            vmem((size, size), BF16),
            vmem((size, size), BF16),
            vmem((size, size), BF16),
            vmem((loads, size), F32),
            vmem((3, wide, wide), BF16),
            vmem((3, wide, wide), BF16),
            vmem((loads, size), F32),
            vmem((loads, size), F32),
            vmem((loads, size), F32),
            vmem((size, loads), F32),
            vmem((steps, 2, 6, loads // 2, face), BF16),
            vmem((steps, 2, 6, loads // 2, face), BF16),
            pltpu.SemaphoreType.DMA((5,)),
            pltpu.SemaphoreType.DMA((steps, 2, 6)),
            pltpu.SemaphoreType.DMA((steps, 2, 6)),
        ],
        compiler_params=pltpu.CompilerParams(
            collective_id=0, has_side_effects=True, vmem_limit_bytes=56000000
        ),
        name="feti",
    )(ordering.reshape(1, size), intact.reshape(1, size), rhs, schur, dual)
    return out.reshape(1, 1, 1, size, loads)


def solution(mesh):
    counts = tuple(mesh.shape[axis] for axis in AXES)
    in_specs = (
        P("gx", "gy", "gz", None, None),
        P("gx", "gy", "gz", None, None),
        P("gx", "gy", "gz", None, None),
        P("gx", "gy", "gz", None),
        P("gx", "gy", "gz", None),
    )
    out_specs = P("gx", "gy", "gz", None, None)
    return jax.shard_map(
        functools.partial(local, counts), mesh=mesh, in_specs=in_specs, out_specs=out_specs, check_vma=False
    )
```
